256 devices in a mesh: table: 16 (over y_lo, x, core), tensor: 2 (over y_hi), dp: 8 (over z).
Axes of the slice: x: 4, y: 4 (y_hi: 2, y_lo: 2; y = y_hi * 2 + y_lo), z: 8, core: 2. Of those that a mesh axis runs over, the one named last changes fastest.
Arguments:
- lookup_ids: int32 [4096, 16, 16], P('dp', 'table'), may hold values from 0 to 4095
- bag_lengths: int32 [4096, 16], P('dp', 'table'), may hold values from 1 to 16
- feature_widths: int32 [16], replicated, may hold values from 32 to 256, as said below
- tables: bfloat16 [16, 4096, 256], P('table', None, 'tensor'), may hold values from -6 to 6
- w_in: bfloat16 [4096, 16384], P(None, ('table', 'tensor')), may hold values from -0.25 to 0.25
- w_out: bfloat16 [16384, 4096], P(('table', 'tensor')), may hold values from -0.1875 to 0.1875
- cotangent: bfloat16 [4096, 4096], P('dp', ('table', 'tensor')), may hold values from -6 to 6
Outputs:
- mixed_out: bfloat16 [4096, 4096], P('dp', ('table', 'tensor'))
- grad_in: float32 [4096, 16384], P('dp', ('table', 'tensor'))
- grad_out: float32 [16384, 4096], P(('table', 'tensor', 'dp'))
The draws below stay inside these ranges and needn't reach their ends.
Inputs may be any that keep to these rules, and one draw needn't show every extreme that they name: `feature_widths`: multiples of 32; one feature has exactly 256, another exactly 32.
All inputs are finite; a program needn't handle non-finite values.
Results may differ from the reference program's by a relative error of at most 0.0056.
Values may be sent and summed in bfloat16 or wider, within the bound.
A program may use at most 128 MiB of HBM per device.

```python
import jax
import jax.numpy as jnp
from jax import lax

EMB = 256
H = 16384
OUT = 4096
VOCAB = 4096
BAG = 16
FEATS = 16
IN = 4096
SAMPLES = 4096


def draw_feature_widths(key, part):
    key_levels = jax.random.fold_in(key, 11)
    key_pick = jax.random.fold_in(key, 23)
    levels = jax.random.randint(key_levels, (FEATS,), 1, 9)
    chosen = jax.random.randint(key_pick, (), 0, FEATS)
    positions = jnp.arange(FEATS)
    levels = jnp.where(positions == chosen, 8, jnp.where(positions == (chosen + 1) % FEATS, 1, levels))
    return (levels * (EMB // 8)).astype(jnp.int32)


def place_ends(result, own_key, low, largest):
    extent = result.shape
    index_at = [jax.random.randint(jax.random.fold_in(own_key, axis), (), 0, extent[axis]) for axis in range(len(extent))]
    result = result.at[tuple(index_at)].set(low)
    longest = extent.index(max(extent))
    index_at[longest] = (index_at[longest] + 1) % extent[longest]
    return result.at[tuple(index_at)].set(largest)


def raised(drawn, rng, source, target, shards_of, factor):
    def block_of(dim):
        return (jnp.arange(drawn.shape[dim]) // (drawn.shape[dim] // shards_of)).reshape((-1,) + (1,) * (drawn.ndim - 1 - dim))

    near = jax.random.permutation(rng, shards_of)[block_of(target)]
    second = (block_of(target) + shards_of // 2) % shards_of
    return jnp.where((block_of(source) == near) | (block_of(source) == second), factor * drawn, drawn)


def level_of(key, shape, shards, least, top_value):
    factor_of = 1.0
    for position, blocks in shards:
        draws = jax.random.uniform(jax.random.fold_in(jax.random.fold_in(key, 6), position), (blocks,), jnp.float32, least / len(shards), top_value / len(shards))
        factor_of = factor_of * jnp.repeat(jnp.exp(draws), shape[position] // blocks).reshape((-1,) + (1,) * (len(shape) - 1 - position))
    return factor_of


def scatter_about(stream_key, extent, scale, bound, cuts=(), held_as=jnp.bfloat16):
    entries = scale * jax.random.normal(stream_key, extent, jnp.float32)
    if cuts:
        entries = entries * level_of(stream_key, extent, cuts, -0.22, 0.18)
    return jnp.clip(entries, -bound, bound).astype(held_as)


def noise_with(stream_key, extent, scale, limit, split, heavy, held_as=jnp.bfloat16):
    entries = scale * jax.random.normal(stream_key, extent, jnp.float32)
    if split:
        entries = entries * level_of(stream_key, extent, split, -0.22, 0.18)
    return jnp.clip(raised(entries, jax.random.fold_in(stream_key, 3), *heavy), -limit, limit).astype(held_as)


def setup_inputs(seed: int = 0) -> dict:
    key_of = jax.random.split(jax.random.key(seed), 8)
    lookup_ids = place_ends(jax.random.randint(key_of[0], (SAMPLES, FEATS, BAG), 0, VOCAB), jax.random.fold_in(key_of[0], 1), 0, VOCAB - 1).astype(jnp.int32)
    bag_lengths = place_ends(jax.random.randint(key_of[1], (SAMPLES, FEATS), 1, BAG + 1), jax.random.fold_in(key_of[1], 1), 1, BAG).astype(jnp.int32)
    feature_widths = draw_feature_widths(jax.random.fold_in(key_of[7], 71), 0)
    tables = scatter_about(key_of[3], (FEATS, VOCAB, EMB), 1.0, 6.0, ((0, 16), (2, 2)))
    w_in = scatter_about(key_of[4], (IN, H), (IN // 8) ** -0.5, 0.25, ((1, 32),))
    w_out = noise_with(key_of[5], (H, OUT), (H // 4) ** -0.5, 0.1875, ((0, 32),), (0, 1, 32, 2.75))
    cotangent = scatter_about(key_of[6], (SAMPLES, OUT), 1.0, 6.0, ((0, 8), (1, 32)))
    return {"lookup_ids": lookup_ids, "bag_lengths": bag_lengths, "feature_widths": feature_widths, "tables": tables, "w_in": w_in, "w_out": w_out, "cotangent": cotangent}


def silu_slope(preact):
    sigmoid_part = jax.nn.sigmoid(preact)
    return sigmoid_part * (1.0 + preact * (1.0 - sigmoid_part))


def pool_feature(inputs):
    lookup, lengths, embedding, width = inputs
    in_bag = jnp.arange(BAG)[None, :] < lengths[:, None]
    vocab_ids = jnp.arange(VOCAB).astype(jnp.int32)
    counts = jnp.zeros((lookup.shape[0], VOCAB), jnp.float32)
    for slot_index in range(BAG):
        hits = (lookup[:, slot_index:slot_index + 1] == vocab_ids[None, :]) & in_bag[:, slot_index:slot_index + 1]
        counts = counts + hits.astype(jnp.float32)
    summed = jnp.dot(counts.astype(jnp.bfloat16), embedding, preferred_element_type=jnp.float32)
    pooled = summed / lengths[:, None].astype(jnp.float32)
    keep = jnp.arange(EMB)[None, :] < width
    return jnp.where(keep, pooled, jnp.zeros_like(pooled)).astype(jnp.bfloat16)


def reference(lookup_ids, bag_lengths, feature_widths, tables, w_in, w_out, cotangent):
    pooled = lax.map(pool_feature, (jnp.transpose(lookup_ids, (1, 0, 2)), jnp.transpose(bag_lengths), tables, feature_widths))
    features = jnp.transpose(pooled, (1, 0, 2)).reshape(SAMPLES, IN)
    preact = jnp.dot(features, w_in, preferred_element_type=jnp.float32)
    hidden = jax.nn.silu(preact).astype(jnp.bfloat16)
    mixed_out = jnp.dot(hidden, w_out, preferred_element_type=jnp.float32).astype(jnp.bfloat16)
    grad_hidden = jnp.dot(cotangent, w_out.T, preferred_element_type=jnp.float32)
    grad_preact = (grad_hidden * silu_slope(preact)).astype(jnp.bfloat16)
    grad_in = jnp.dot(features.T, grad_preact, preferred_element_type=jnp.float32)
    grad_out = jnp.dot(hidden.T, cotangent, preferred_element_type=jnp.float32)
    return (mixed_out, grad_in, grad_out)
```

```python
import functools

import jax
import jax.numpy as jnp
from jax import lax
from jax.experimental import pallas as pl
from jax.experimental.pallas import tpu as pltpu
from jax.sharding import PartitionSpec as P

MESH = pl.DeviceIdType.MESH
F32, BF16 = jnp.float32, jnp.bfloat16
SIDE = 4
DEPTH = 8
LANES = 128
TILE = 512
VOCAB_STEP = 256


def mul128(i):
    return pl.multiple_of(i * LANES, LANES)


def kernel(
    widths, ids, lens, table_hbm, w_in_hbm, w_out_hbm, cot_hbm,
    mixed, grad_in, grad_out,
    table, w_in, w_out, cot, feat, wide, counts, pooled, gh, pre, hid, hid_t, gp,
    part, pair, st1, st2, row_sum, z_in, z_out,
    in_sem, ag_send, ag_recv, rs_send, rs_recv, z_send, z_recv,
):
    t, yh, z = lax.axis_index("table"), lax.axis_index("tensor"), lax.axis_index("dp")
    core = lax.rem(t, 2)
    x = lax.rem(lax.div(t, 2), SIDE)
    y = yh * 2 + lax.div(t, 2 * SIDE)
    turn = 1 - 2 * core
    samples, bag = ids.shape
    half = samples // 2

    def ring(i):
        return lax.rem(i + 2 * SIDE, SIDE)

    def ring_z(i):
        return lax.rem(i + 2 * DEPTH, DEPTH)

    def dev(px, py, c, pz):
        return {"table": (lax.rem(py, 2) * SIDE + px) * 2 + c, "tensor": lax.div(py, 2), "dp": pz}

    def block(px, py, c):
        return ((lax.rem(py, 2) * SIDE + px) * 2 + c) * 2 + lax.div(py, 2)

    def place(h, a, b):
        return (a, b) if h == 0 else (b, a)

    first = (x, y)
    second = (y, x)

    def peer(h, a, b):
        px, py = place(h, a, b)
        return dev(px, py, core, z)

    partner = dev(x, y, 1 - core, z)

    loads = [
        pltpu.make_async_copy(cot_hbm, cot.at[:, pl.ds(mul128(block(x, y, core)), LANES)], in_sem.at[0]),
        pltpu.make_async_copy(table_hbm, table, in_sem.at[1]),
        pltpu.make_async_copy(w_out_hbm, w_out, in_sem.at[2]),
        pltpu.make_async_copy(w_in_hbm, w_in, in_sem.at[3]),
    ]
    for load in loads:
        load.start()

    barrier = pltpu.get_barrier_semaphore()
    neighbours = [
        dev(ring(x + 1), y, core, z), dev(ring(x - 1), y, core, z),
        dev(x, ring(y + 1), core, z), dev(x, ring(y - 1), core, z),
        dev(x, y, core, ring_z(z + 1)), dev(x, y, core, ring_z(z - 1)), partner,
    ]
    for neighbour in neighbours:
        pl.semaphore_signal(barrier, inc=1, device_id=neighbour, device_id_type=MESH)
    pl.semaphore_wait(barrier, len(neighbours))

    def remote(src, dst, s, r, to):
        return pltpu.make_async_remote_copy(
            src_ref=src, dst_ref=dst, send_sem=s, recv_sem=r, device_id=to, device_id_type=MESH
        )

    sends = []

    def gather(which, buf):
        def view(h, a, b, c):
            px, py = place(h, a, b)
            return buf.at[pl.ds(h * half, half), pl.ds(mul128(block(px, py, c)), LANES)]

        def base(h):
            return (which * 2 + h) * 31

        def copy(h, a, b, slot, recv_slot, to):
            ref = view(h, a, b, core)
            c = remote(ref, ref, ag_send.at[base(h) + slot], ag_recv.at[base(h) + recv_slot], to)
            c.start()
            sends.append(c)

        def arrived(h, a, b, recv_slot, c):
            ref = view(h, a, b, c)
            remote(ref, ref, ag_send.at[base(h)], ag_recv.at[base(h) + recv_slot], partner).wait_recv()

        def to_partner(h, a, b, n):
            copy(h, a, b, 15 + n, 15 + n, partner)

        def offset(j):
            return (0, -turn, turn, 2)[j]

        def line(h, j):
            a, b = first[h], second[h]
            aj = ring(a + offset(j))
            copy(h, aj, b, 3 + 3 * j, 3 + 3 * j + core, peer(h, a, ring(b + turn)))
            copy(h, aj, b, 4 + 3 * j, 3 + 3 * j + (1 - core), peer(h, a, ring(b - turn)))

        def begin():
            for h in range(2):
                a, b = first[h], second[h]
                copy(h, a, b, 0, core, peer(h, ring(a + turn), b))
                copy(h, a, b, 1, 1 - core, peer(h, ring(a - turn), b))
            for h in range(2):
                line(h, 0)
                to_partner(h, first[h], second[h], 0)

        def near(h):
            a, b = first[h], second[h]
            aj = ring(a - turn)
            arrived(h, aj, b, core, core)
            copy(h, aj, b, 2, 2, peer(h, ring(a + turn), b))
            line(h, 1)
            to_partner(h, aj, b, 1)

        def other(h):
            a, b = first[h], second[h]
            aj = ring(a + turn)
            arrived(h, aj, b, 1 - core, core)
            line(h, 2)
            to_partner(h, aj, b, 2)

        def far(h):
            a, b = first[h], second[h]
            aj = ring(a + 2)
            arrived(h, aj, b, 2, core)
            line(h, 3)
            to_partner(h, aj, b, 3)

        def cross(h, j):
            a, b = first[h], second[h]
            aj = ring(a + offset(j))
            bj = ring(b - turn)
            arrived(h, aj, bj, 3 + 3 * j + core, core)
            copy(h, aj, bj, 5 + 3 * j, 5 + 3 * j, peer(h, a, ring(b + turn)))
            to_partner(h, aj, bj, 4 + 3 * j)
            bj = ring(b + turn)
            arrived(h, aj, bj, 3 + 3 * j + (1 - core), core)
            to_partner(h, aj, bj, 5 + 3 * j)

        def cross_far(h, j):
            a, b = first[h], second[h]
            aj, bj = ring(a + offset(j)), ring(b + 2)
            arrived(h, aj, bj, 5 + 3 * j, core)
            to_partner(h, aj, bj, 6 + 3 * j)

        def partner_in(h):
            a, b = first[h], second[h]
            for n in range(16):
                if n < 4:
                    aj, bj = ring(a + (0, turn, -turn, 2)[n]), b
                else:
                    j, k = divmod(n - 4, 3)
                    aj = ring(a + (0, turn, -turn, 2)[j])
                    bj = ring(b + (turn, -turn, 2)[k])
                arrived(h, aj, bj, 15 + n, 1 - core)

        steps = [
            lambda: (near(0), near(1)),
            lambda: (other(0), other(1)),
            lambda: (far(0), far(1)),
            lambda: (cross(0, 0), cross(1, 0)),
            lambda: (cross(0, 1), cross(1, 1)),
            lambda: (cross(0, 2), cross(1, 2)),
            lambda: (cross(0, 3), cross(1, 3)),
            lambda: [cross_far(h, j) for j in range(4) for h in range(2)],
            lambda: (partner_in(0), partner_in(1)),
        ]
        return begin, steps

    def spread():
        inside = lax.broadcasted_iota(jnp.int32, (samples, bag), 1) < lens[...]
        masked = jnp.where(inside, ids[...], -1)
        for b in range(bag):
            wide[b] = jnp.broadcast_to(masked[:, b : b + 1], (samples, LANES)).astype(jnp.int16)

    def pool(low, high):
        rows = 64

        @pl.loop(low, high)
        def _(v):
            start = v * VOCAB_STEP
            for piece in range(VOCAB_STEP // LANES):
                target = (
                    lax.broadcasted_iota(jnp.int32, (rows, LANES), 1) + (start + piece * LANES)
                ).astype(jnp.int16)
                for r in range(0, samples, rows):
                    total = jnp.zeros((rows, LANES), BF16)
                    for b in range(bag):
                        hit = wide[b, r : r + rows, :] == target
                        total = total + jnp.where(hit, jnp.ones((), BF16), jnp.zeros((), BF16))
                    counts[r : r + rows, piece * LANES : (piece + 1) * LANES] = total
            picked = table[pl.ds(pl.multiple_of(start, VOCAB_STEP), VOCAB_STEP), :]
            pooled[...] += jnp.dot(counts[...], picked, preferred_element_type=F32)

    def pool_end():
        mean = pooled[...] / lens[...].astype(F32)
        column = lax.broadcasted_iota(jnp.int32, (samples, LANES), 1) + yh * LANES
        mean = jnp.where(column < widths[t], mean, jnp.zeros_like(mean))
        feat[:, pl.ds(mul128(block(x, y, core)), LANES)] = mean.astype(BF16)

    def grad_hidden(low, high):
        @pl.loop(low, high)
        def _(k):
            cols = pl.ds(pl.multiple_of(k * TILE, TILE), TILE)
            gh[...] += lax.dot_general(
                cot[:, cols], w_out[:, cols], (((1,), (1,)), ((), ())), preferred_element_type=F32
            )

    def preact():
        @pl.loop(0, feat.shape[1] // TILE)
        def _(k):
            cols = pl.ds(pl.multiple_of(k * TILE, TILE), TILE)
            pre[...] += jnp.dot(feat[:, cols], w_in[cols, :], preferred_element_type=F32)

    begin_cot, cot_steps = gather(0, cot)
    begin_feat, feat_steps = gather(1, feat)
    loads[0].wait()
    begin_cot()
    spread()
    pooled[...] = jnp.zeros_like(pooled)
    gh[...] = jnp.zeros_like(gh)
    pre[...] = jnp.zeros_like(pre)
    loads[1].wait()
    blocks = table.shape[0] // VOCAB_STEP
    quarter = blocks // 4
    for q in range(4):
        pool(q * quarter, (q + 1) * quarter)
        if q < 3:
            cot_steps[q]()
    pool_end()
    begin_feat()
    cot_steps[3]()
    cot_steps[4]()
    feat_steps[0]()
    cot_steps[5]()
    feat_steps[1]()
    cot_steps[6]()
    feat_steps[2]()
    cot_steps[7]()
    feat_steps[3]()
    cot_steps[8]()
    loads[2].wait()
    tiles = cot.shape[1] // TILE
    for q in range(4):
        grad_hidden(q * tiles // 4, (q + 1) * tiles // 4)
        feat_steps[4 + q]()
    loads[3].wait()
    feat_steps[8]()
    preact()

    rows = 64

    @pl.loop(0, samples // rows)
    def _(i):
        r = pl.ds(pl.multiple_of(i * rows, rows), rows)
        value = pre[r, :]
        gate = jax.nn.sigmoid(value)
        hid[r, :] = (value * gate).astype(BF16)
        gp[r, :] = (gh[r, :] * (gate * (1.0 + value * (1.0 - gate)))).astype(BF16)

    hid_t[...] = jnp.transpose(hid[...])

    in_rows, in_cols = grad_in.shape
    out_rows, out_cols = grad_out.shape

    def add_in(d, terms, store):
        step = 128

        @pl.loop(0, in_rows // step)
        def _(i):
            r = pl.ds(pl.multiple_of(i * step, step), step)
            cols = pl.ds(pl.multiple_of(d * in_rows + i * step, step), step)
            own = lax.dot_general(feat[:, cols], gp[...], (((0,), (0,)), ((), ())), preferred_element_type=F32)
            for term in terms:
                own = own + term[r, :].astype(F32)
            store[r, :] = own.astype(store.dtype)

    def add_out(d, terms, store):
        @pl.loop(0, out_cols // TILE)
        def _(j):
            cols = pl.ds(pl.multiple_of(j * TILE, TILE), TILE)
            lhs = hid_t[pl.ds(pl.multiple_of(d * out_rows, out_rows), out_rows), :]
            own = jnp.dot(lhs, cot[:, cols], preferred_element_type=F32)
            for term in terms:
                own = own + term[:, cols].astype(F32)
            store[:, cols] = own.astype(store.dtype)

    up, down = dev(x, y, core, ring_z(z + 1)), dev(x, y, core, ring_z(z - 1))
    chains = {"in+": (0, 4, 1), "in-": (4, 3, -1), "out+": (0, 3, 1), "out-": (3, 4, -1)}

    def z_copy(name, s):
        slot, hops, sign = chains[name]
        slots, starts = (z_in, 0) if name[:2] == "in" else (z_out, 7)
        first_slot = 7 + (0 if sign > 0 else 1)
        src = slots.at[first_slot] if s == 0 else slots.at[slot + s - 1]
        sem = starts + slot + s
        return remote(src, slots.at[slot + s], z_send.at[sem], z_recv.at[sem], up if sign > 0 else down)

    def z_step(name, s):
        slot, hops, sign = chains[name]
        slots = z_in if name[:2] == "in" else z_out
        add = add_in if name[:2] == "in" else add_out
        d = ring_z(z + sign * (hops - s))
        if s == 0:
            add(d, [], slots.at[7 + (0 if sign > 0 else 1)])
        else:
            z_copy(name, s - 1).wait_recv()
            add(d, [slots.at[slot + s - 1]], slots.at[slot + s - 1])
        c = z_copy(name, s)
        c.start()
        sends.append(c)

    def rs(h, n, src, dst, to):
        i = h * 15 + n
        c = remote(src, dst, rs_send.at[i], rs_recv.at[i], to)
        c.start()
        sends.append(c)

    def rs_wait(h, n, ref):
        i = h * 15 + n
        remote(ref, ref, rs_send.at[i], rs_recv.at[i], partner).wait_recv()

    def cols_of(px, py, c):
        return pl.ds(mul128(block(px, py, c)), LANES)

    def out_partial():
        @pl.loop(0, part.shape[1] // TILE)
        def _(j):
            cols = pl.ds(pl.multiple_of(j * TILE, TILE), TILE)
            part[:, cols] = jnp.dot(hid[...], w_out[:, cols], preferred_element_type=F32).astype(BF16)

    def pair_copy(n):
        px, py = divmod(n, SIDE)
        return remote(
            part.at[:, cols_of(px, py, 1 - core)], pair.at[n], rs_send.at[30 + n], rs_recv.at[30 + n], partner
        )

    def pair_send():
        for n in range(SIDE * SIDE):
            c = pair_copy(n)
            c.start()
            sends.append(c)

    def pair_add():
        for n in range(SIDE * SIDE):
            pair_copy(n).wait_recv()

        @pl.loop(0, SIDE * SIDE)
        def _(n):
            px, py = lax.div(n, SIDE), lax.rem(n, SIDE)
            both = part[:, cols_of(px, py, core)].astype(F32) + pair[n].astype(F32)
            pair[n] = both.astype(BF16)

    def chip(h, a, b):
        px, py = (b, a) if h == 0 else (a, b)
        return pair.at[px * SIDE + py, pl.ds(h * half, half), :]

    def along(h, da, db):
        if h == 0:
            return dev(ring(x + db), ring(y + da), core, z)
        return dev(ring(x + da), ring(y + db), core, z)

    def axes(h):
        return (y, x) if h == 0 else (x, y)

    def rs_first():
        for h in range(2):
            a, b = axes(h)
            for k in range(SIDE):
                rs(h, k, chip(h, ring(a + 2), k), st1.at[h, 0, k], along(h, turn, 0))
                rs(h, 4 + k, chip(h, ring(a - turn), k), st1.at[h, 1, k], along(h, -turn, 0))

    def rs_second():
        for h in range(2):
            a, b = axes(h)
            for k in range(SIDE):
                rs_wait(h, k, st1.at[h, 0, k])
                own = chip(h, ring(a + turn), k)[...].astype(F32)
                st1[h, 0, k] = (own + st1[h, 0, k].astype(F32)).astype(BF16)
                rs(h, 8 + k, st1.at[h, 0, k], st1.at[h, 2, k], along(h, turn, 0))

    def rs_third():
        for h in range(2):
            a, b = axes(h)
            for k in range(SIDE):
                rs_wait(h, 4 + k, st1.at[h, 1, k])
                rs_wait(h, 8 + k, st1.at[h, 2, k])
                own = chip(h, a, k)[...].astype(F32)
                row_sum[h, k] = own + st1[h, 1, k].astype(F32) + st1[h, 2, k].astype(F32)
            st2[h, 3] = row_sum[h, ring(b + 2)].astype(BF16)
            rs(h, 12, st2.at[h, 3], st2.at[h, 0], along(h, 0, turn))
            st2[h, 4] = row_sum[h, ring(b - turn)].astype(BF16)
            rs(h, 13, st2.at[h, 4], st2.at[h, 1], along(h, 0, -turn))

    def rs_fourth():
        for h in range(2):
            a, b = axes(h)
            rs_wait(h, 12, st2.at[h, 0])
            st2[h, 5] = (row_sum[h, ring(b + turn)] + st2[h, 0].astype(F32)).astype(BF16)
            rs(h, 14, st2.at[h, 5], st2.at[h, 2], along(h, 0, turn))

    def rs_last():
        for h in range(2):
            a, b = axes(h)
            rs_wait(h, 13, st2.at[h, 1])
            rs_wait(h, 14, st2.at[h, 2])
            total = row_sum[h, b] + st2[h, 1].astype(F32) + st2[h, 2].astype(F32)
            mixed[h * half : (h + 1) * half, :] = total.astype(BF16)

    z_step("in+", 0)
    z_step("out-", 0)
    z_step("out+", 0)
    z_step("in-", 0)
    out_partial()
    pair_send()
    pair_add()
    rs_first()
    z_step("in+", 1)
    z_step("out-", 1)
    rs_second()
    z_step("out+", 1)
    z_step("in-", 1)
    rs_third()
    z_step("in+", 2)
    z_step("out-", 2)
    rs_fourth()
    z_step("out+", 2)
    z_step("in-", 2)
    rs_last()
    z_step("in+", 3)
    z_step("out-", 3)
    for name in ("out+", "in-", "in+", "out-"):
        slot, hops, sign = chains[name]
        z_copy(name, hops - 1).wait_recv()
        if name == "in+":
            add_in(z, [z_in.at[3], z_in.at[6]], grad_in)
        if name == "out-":
            add_out(z, [z_out.at[2], z_out.at[6]], grad_out)
    for c in sends:
        c.wait_send()


def shards(lookup_ids, bag_lengths, feature_widths, tables, w_in, w_out, cotangent):
    samples, bag = lookup_ids.shape[0], lookup_ids.shape[2]
    vocab = tables.shape[1]
    wide_in, hidden = w_in.shape
    wide_out = w_out.shape[1]
    in_rows, out_rows = wide_in // DEPTH, hidden // DEPTH
    half = samples // 2
    vmem = pl.BlockSpec(memory_space=pltpu.VMEM)
    hbm = pl.BlockSpec(memory_space=pl.ANY)
    dma = pltpu.SemaphoreType.DMA
    return pl.pallas_call(
        kernel,
        out_shape=(
            jax.ShapeDtypeStruct((samples, LANES), BF16),
            jax.ShapeDtypeStruct((in_rows, hidden), F32),
            jax.ShapeDtypeStruct((out_rows, wide_out), F32),
        ),
        in_specs=[pl.BlockSpec(memory_space=pltpu.SMEM), vmem, vmem, hbm, hbm, hbm, hbm],
        out_specs=(vmem, vmem, vmem),
        scratch_shapes=[
            pltpu.VMEM((vocab, LANES), BF16),
            pltpu.VMEM((wide_in, hidden), BF16),
            pltpu.VMEM((hidden, wide_out), BF16),
            pltpu.VMEM((samples, wide_out), BF16),
            pltpu.VMEM((samples, wide_in), BF16),
            pltpu.VMEM((bag, samples, LANES), jnp.int16),
            pltpu.VMEM((samples, VOCAB_STEP), BF16),
            pltpu.VMEM((samples, LANES), F32),
            pltpu.VMEM((samples, hidden), F32),
            pltpu.VMEM((samples, hidden), F32),
            pltpu.VMEM((samples, hidden), BF16),
            pltpu.VMEM((hidden, samples), BF16),
            pltpu.VMEM((samples, hidden), BF16),
            pltpu.VMEM((samples, wide_out), BF16),
            pltpu.VMEM((SIDE * SIDE, samples, LANES), BF16),
            pltpu.VMEM((2, 3, SIDE, half, LANES), BF16),
            pltpu.VMEM((2, 6, half, LANES), BF16),
            pltpu.VMEM((2, SIDE, half, LANES), F32),
            pltpu.VMEM((9, in_rows, hidden), BF16),
            pltpu.VMEM((9, out_rows, wide_out), BF16),
            dma((4,)),
            dma((124,)),
            dma((124,)),
            dma((46,)),
            dma((46,)),
            dma((14,)),
            dma((14,)),
        ],
        compiler_params=pltpu.CompilerParams(
            collective_id=0, has_side_effects=True, vmem_limit_bytes=63 * 1024 * 1024
        ),
    )(feature_widths, lookup_ids[:, 0, :], bag_lengths, tables[0], w_in, w_out, cotangent)


def solution(mesh):
    return jax.shard_map(
        shards,
        mesh=mesh,
        in_specs=(
            P("dp", "table", None),
            P("dp", "table"),
            P(),
            P("table", None, "tensor"),
            P(None, ("table", "tensor")),
            P(("table", "tensor"), None),
            P("dp", ("table", "tensor")),
        ),
        out_specs=(
            P("dp", ("table", "tensor")),
            P("dp", ("table", "tensor")),
            P(("table", "tensor", "dp"), None),
        ),
        check_vma=False,
    )
```

```python
import functools

import jax
import jax.numpy as jnp
from jax import lax
from jax.experimental import pallas as pl
from jax.experimental.pallas import tpu as pltpu
from jax.sharding import PartitionSpec as P

MESH = pl.DeviceIdType.MESH
F32, BF16 = jnp.float32, jnp.bfloat16
SIDE = 4
DEPTH = 8
LANES = 128
TILE = 512
PLAN_BEFORE = ((), (), (), (0, 1), (), (2,), (3,), ())
PLAN_AFTER = ((0, 4), (1, 0), (0, 5), (1, 1), (0, 6), (1, 2), (1, 3), (0, 7), (1, 4), (1, 5), (1, 6), (0, 8), (1, 7))
PIECES = 8
FIELDS = 4


def mul128(i):
    return pl.multiple_of(i * LANES, LANES)


def kernel(
    widths, ids, lens, table_hbm, w_in_hbm, w_out_hbm, cot_hbm,
    mixed, grad_in, grad_out,
    table, w_in, w_out, cot, feat, keys, spans, counts, gh, pre, hid, hid_t, gp,
    part, pair, st1, st2, row_sum, z_in, z_out,
    in_sem, ag_send, ag_recv, rs_send, rs_recv, z_send, z_recv,
):
    t, yh, z = lax.axis_index("table"), lax.axis_index("tensor"), lax.axis_index("dp")
    core = lax.rem(t, 2)
    x = lax.rem(lax.div(t, 2), SIDE)
    y = yh * 2 + lax.div(t, 2 * SIDE)
    turn = 1 - 2 * core
    bag, samples = ids.shape
    half = samples // 2

    def ring(i):
        return lax.rem(i + 2 * SIDE, SIDE)

    def ring_z(i):
        return lax.rem(i + 2 * DEPTH, DEPTH)

    def dev(px, py, c, pz):
        return {"table": (lax.rem(py, 2) * SIDE + px) * 2 + c, "tensor": lax.div(py, 2), "dp": pz}

    def block(px, py, c):
        return ((lax.rem(py, 2) * SIDE + px) * 2 + c) * 2 + lax.div(py, 2)

    def place(h, a, b):
        return (a, b) if h == 0 else (b, a)

    first = (x, y)
    second = (y, x)

    def peer(h, a, b):
        px, py = place(h, a, b)
        return dev(px, py, core, z)

    partner = dev(x, y, 1 - core, z)

    loads = [
        pltpu.make_async_copy(cot_hbm, cot.at[:, pl.ds(mul128(block(x, y, core)), LANES)], in_sem.at[0]),
        pltpu.make_async_copy(table_hbm, table, in_sem.at[1]),
        pltpu.make_async_copy(w_out_hbm, w_out, in_sem.at[2]),
        pltpu.make_async_copy(w_in_hbm, w_in, in_sem.at[3]),
    ]
    for load in loads:
        load.start()

    barrier = pltpu.get_barrier_semaphore()
    neighbours = [
        dev(ring(x + 1), y, core, z), dev(ring(x - 1), y, core, z),
        dev(x, ring(y + 1), core, z), dev(x, ring(y - 1), core, z),
        dev(x, y, core, ring_z(z + 1)), dev(x, y, core, ring_z(z - 1)), partner,
    ]
    for neighbour in neighbours:
        pl.semaphore_signal(barrier, inc=1, device_id=neighbour, device_id_type=MESH)

    def remote(src, dst, s, r, to):
        return pltpu.make_async_remote_copy(
            src_ref=src, dst_ref=dst, send_sem=s, recv_sem=r, device_id=to, device_id_type=MESH
        )

    def gather(which, buf, row, rows):
        def view(h, a, b, c):
            px, py = place(h, a, b)
            return buf.at[pl.ds(row + h * (rows // 2), rows // 2), pl.ds(mul128(block(px, py, c)), LANES)]

        def copy(h, a, b, recv_slot, to):
            ref = view(h, a, b, core)
            remote(ref, ref, ag_send.at[which], ag_recv.at[which * 16 + recv_slot], to).start()

        def arrived(recv_slot, blocks=1):
            ref = buf.at[:rows, : blocks * LANES]
            remote(ref, ref, ag_send.at[which], ag_recv.at[which * 16 + recv_slot], partner).wait_recv()

        def sent():
            ref = buf.at[:rows, : 31 * LANES]
            remote(ref, ref, ag_send.at[which], ag_recv.at[which * 16], partner).wait_send()

        def to_partner(h, a, b):
            copy(h, a, b, 15, partner)

        def offset(j):
            return (0, -turn, turn, 2)[j]

        def line(h, j):
            a, b = first[h], second[h]
            aj = ring(a + offset(j))
            copy(h, aj, b, 3 + 3 * j + core, peer(h, a, ring(b + turn)))
            copy(h, aj, b, 3 + 3 * j + (1 - core), peer(h, a, ring(b - turn)))

        def begin():
            for h in range(2):
                a, b = first[h], second[h]
                copy(h, a, b, core, peer(h, ring(a + turn), b))
                copy(h, a, b, 1 - core, peer(h, ring(a - turn), b))
            for h in range(2):
                line(h, 0)
                to_partner(h, first[h], second[h])

        def near():
            arrived(core)
            for h in range(2):
                a, b = first[h], second[h]
                aj = ring(a - turn)
                copy(h, aj, b, 2, peer(h, ring(a + turn), b))
                line(h, 1)
                to_partner(h, aj, b)

        def other():
            arrived(1 - core)
            for h in range(2):
                line(h, 2)
                to_partner(h, ring(first[h] + turn), second[h])

        def far():
            arrived(2)
            for h in range(2):
                line(h, 3)
                to_partner(h, ring(first[h] + 2), second[h])

        def cross(j):
            arrived(3 + 3 * j + core)
            for h in range(2):
                a, b = first[h], second[h]
                aj, bj = ring(a + offset(j)), ring(b - turn)
                copy(h, aj, bj, 5 + 3 * j, peer(h, a, ring(b + turn)))
                to_partner(h, aj, bj)
            arrived(3 + 3 * j + (1 - core))
            for h in range(2):
                to_partner(h, ring(first[h] + offset(j)), ring(second[h] + turn))

        def cross_far(j):
            arrived(5 + 3 * j)
            for h in range(2):
                to_partner(h, ring(first[h] + offset(j)), ring(second[h] + 2))

        steps = [
            near,
            other,
            far,
            lambda: cross(0),
            lambda: cross(1),
            lambda: cross(2),
            lambda: cross(3),
            lambda: [cross_far(j) for j in range(4)],
            lambda: arrived(15, 16),
        ]
        return begin, steps, sent

    vocab = table.shape[0]
    words = vocab // FIELDS

    def spread():
        inside = lax.broadcasted_iota(jnp.int32, (bag, samples), 0) < lens[...]
        field = lax.shift_right_logical(ids[...], words.bit_length() - 1)
        code = lax.bitwise_and(ids[...], words - 1) + field * (8 << 16)
        keys[...] = jnp.transpose(jnp.where(inside, code, 2 * words))

        spans[...] = jnp.transpose(jnp.broadcast_to(lens[...], (8, samples)).astype(F32))

    piece = counts.shape[1]

    def count(n):
        rows = 8
        lane = lax.broadcasted_iota(jnp.int32, (rows, LANES), 1)
        for g in range(0, piece, rows):
            code = keys[n * piece + g : n * piece + g + rows, :]
            spread_keys, spread_units = [], []
            for b in range(bag):
                wide = jnp.broadcast_to(code[:, b : b + 1], (rows, LANES))
                spread_keys.append(lax.bitwise_and(wide, 0xFFFF))
                spread_units.append(lax.shift_left(jnp.ones_like(wide), lax.shift_right_logical(wide, 16)))
            for w in range(0, words, LANES):
                target = lane + w
                parts = []
                for b in range(bag):
                    parts.append(jnp.where(spread_keys[b] == target, spread_units[b], 0))
                while len(parts) > 1:
                    parts = [p + q for p, q in zip(parts[::2], parts[1::2])]
                for f in range(FIELDS):
                    number = lax.bitwise_and(lax.shift_right_logical(parts[0], 8 * f), 255)
                    at = f * words + w
                    counts[n % 2, g : g + rows, at : at + LANES] = number.astype(F32).astype(BF16)

    def pool_end(n):
        r = slice(n * piece, (n + 1) * piece)
        summed = jnp.dot(counts[n % 2], table[...], preferred_element_type=F32)
        mean = summed / spans[r, 0:1]
        column = lax.broadcasted_iota(jnp.int32, (piece, LANES), 1) + yh * LANES
        mean = jnp.where(column < widths[t], mean, jnp.zeros_like(mean))
        feat[r, pl.ds(mul128(block(x, y, core)), LANES)] = mean.astype(BF16)

    def grad_hidden(low, high):
        @pl.loop(low, high)
        def _(k):
            cols = pl.ds(pl.multiple_of(k * TILE, TILE), TILE)
            gh[...] += lax.dot_general(
                cot[:, cols], w_out[:, cols], (((1,), (1,)), ((), ())), preferred_element_type=F32
            )

    def preact(parity):
        width = 4 * LANES // 2

        @pl.loop(0, feat.shape[1] // (2 * width))
        def _(k):
            cols = pl.ds(pl.multiple_of((2 * k + parity) * width, width), width)
            pre[...] += jnp.dot(feat[:, cols], w_in[cols, :], preferred_element_type=F32)

    begin_cot, cot_steps, cot_sent = gather(0, cot, 0, samples)
    begin_feat, feat_steps, feat_sent = gather(1, feat, 0, samples)
    tiles = cot.shape[1] // TILE
    spread()
    gh[...] = jnp.zeros_like(gh)
    pre[...] = jnp.zeros_like(pre)
    for n in range(PIECES):
        count(n)
        if n == 0:
            loads[1].wait()
            pl.semaphore_wait(barrier, len(neighbours))
            loads[0].wait()
            begin_cot()
        else:
            pool_end(n - 1)
        for k in PLAN_BEFORE[n]:
            cot_steps[k]()
    pool_end(PIECES - 1)
    begin_feat()
    loads[2].wait()
    for which, n in PLAN_AFTER:
        (cot_steps, feat_steps)[which][n]()
    loads[3].wait()
    preact(core)
    feat_steps[8]()
    preact(1 - core)

    rows = 64

    @pl.loop(0, samples // rows)
    def _(i):
        r = pl.ds(pl.multiple_of(i * rows, rows), rows)
        value = pre[r, :]
        gate = jax.nn.sigmoid(value)
        hid[r, :] = (value * gate).astype(BF16)
        pre[r, :] = gate * (1.0 + value * (1.0 - gate))

    hid_t[...] = jnp.transpose(hid[...])

    def grad_preact():
        grad_hidden(0, tiles)

        @pl.loop(0, samples // rows)
        def _(i):
            r = pl.ds(pl.multiple_of(i * rows, rows), rows)
            gp[r, :] = (gh[r, :] * pre[r, :]).astype(BF16)

    in_rows, in_cols = grad_in.shape
    out_rows, out_cols = grad_out.shape

    def add_in(d, terms, store, low, high):
        step = 128

        @pl.loop(low // step, high // step)
        def _(i):
            r = pl.ds(pl.multiple_of(i * step, step), step)
            cols = pl.ds(pl.multiple_of(d * in_rows + i * step, step), step)
            own = lax.dot_general(feat[:, cols], gp[...], (((0,), (0,)), ((), ())), preferred_element_type=F32)
            for term in terms:
                own = own + term[r, :].astype(F32)
            store[r, :] = own.astype(store.dtype)

    def add_out(d, terms, store):
        @pl.loop(0, out_cols // TILE)
        def _(j):
            cols = pl.ds(pl.multiple_of(j * TILE, TILE), TILE)
            lhs = hid_t[pl.ds(pl.multiple_of(d * out_rows, out_rows), out_rows), :]
            own = jnp.dot(lhs, cot[:, cols], preferred_element_type=F32)
            for term in terms:
                own = own + term[:, cols].astype(F32)
            store[:, cols] = own.astype(store.dtype)

    up, down = dev(x, y, core, ring_z(z + 1)), dev(x, y, core, ring_z(z - 1))
    chains = {"out+": (0, 4, 1), "out-": (4, 3, -1), "in+": (0, 3, 1), "in-": (3, 4, -1)}
    in_half = in_rows // 2

    def start_slot(name):
        return 7 + (0 if name.endswith("+") else 1)

    def z_copy(name, s, n=0):
        slot, hops, sign = chains[name]
        from_slot = start_slot(name) if s == 0 else slot + s - 1
        to = up if sign > 0 else down
        if name[:3] == "out":
            return remote(z_out.at[from_slot], z_out.at[slot + s], z_send.at[1], z_recv.at[14 + slot + s], to)
        r = pl.ds(n * in_half, in_half)
        return remote(z_in.at[from_slot, r], z_in.at[slot + s, r], z_send.at[0], z_recv.at[n * 7 + slot + s], to)

    def z_step(name, s):
        slot, hops, sign = chains[name]
        d = ring_z(z + sign * (hops - s))
        for n in range(1 if name[:3] == "out" else 2):
            if s > 0:
                z_copy(name, s - 1, n).wait_recv()
            from_slot = start_slot(name) if s == 0 else slot + s - 1
            slots = z_out if name[:3] == "out" else z_in
            terms = [slots.at[from_slot]] if s > 0 else []
            if name[:3] == "out":
                add_out(d, terms, slots.at[from_slot])
            else:
                add_in(d, terms, slots.at[from_slot], n * in_half, (n + 1) * in_half)
            z_copy(name, s, n).start()

    def rs(h, n, src, dst, to):
        remote(src, dst, rs_send.at[0], rs_recv.at[h * 6 + n], to).start()

    def rs_wait(h, n, ref):
        remote(ref, ref, rs_send.at[0], rs_recv.at[h * 6 + n], partner).wait_recv()

    def cols_of(px, py, c):
        return pl.ds(mul128(block(px, py, c)), LANES)

    def out_partial():
        @pl.loop(0, part.shape[1] // TILE)
        def _(j):
            cols = pl.ds(pl.multiple_of(j * TILE, TILE), TILE)
            part[:, cols] = jnp.dot(hid[...], w_out[:, cols], preferred_element_type=F32).astype(BF16)

    def pair_send():
        for n in range(SIDE * SIDE):
            px, py = divmod(n, SIDE)
            remote(part.at[:, cols_of(px, py, 1 - core)], pair.at[n], rs_send.at[1], rs_recv.at[12], partner).start()

    def pair_add():
        remote(pair, pair, rs_send.at[1], rs_recv.at[12], partner).wait_recv()

        @pl.loop(0, SIDE * SIDE)
        def _(n):
            px, py = lax.div(n, SIDE), lax.rem(n, SIDE)
            both = part[:, cols_of(px, py, core)].astype(F32) + pair[n].astype(F32)
            pair[n] = both.astype(BF16)

    def chip(h, a, b):
        px, py = (b, a) if h == 0 else (a, b)
        return pair.at[px * SIDE + py, pl.ds(h * half, half), :]

    def along(h, da, db):
        if h == 0:
            return dev(ring(x + db), ring(y + da), core, z)
        return dev(ring(x + da), ring(y + db), core, z)

    def axes(h):
        return (y, x) if h == 0 else (x, y)

    def rs_first():
        for h in range(2):
            a, b = axes(h)
            for k in range(SIDE):
                rs(h, 0, chip(h, ring(a + 2), k), st1.at[h, 0, k], along(h, turn, 0))
                rs(h, 1, chip(h, ring(a - turn), k), st1.at[h, 1, k], along(h, -turn, 0))

    def rs_second():
        for h in range(2):
            a, b = axes(h)
            rs_wait(h, 0, st1.at[h, 0])
            for k in range(SIDE):
                own = chip(h, ring(a + turn), k)[...].astype(F32)
                st1[h, 0, k] = (own + st1[h, 0, k].astype(F32)).astype(BF16)
                rs(h, 2, st1.at[h, 0, k], st1.at[h, 2, k], along(h, turn, 0))

    def rs_third():
        for h in range(2):
            a, b = axes(h)
            rs_wait(h, 1, st1.at[h, 1])
            rs_wait(h, 2, st1.at[h, 2])
            for k in range(SIDE):
                own = chip(h, a, k)[...].astype(F32)
                row_sum[h, k] = own + st1[h, 1, k].astype(F32) + st1[h, 2, k].astype(F32)
            st2[h, 3] = row_sum[h, ring(b + 2)]
            rs(h, 3, st2.at[h, 3], st2.at[h, 0], along(h, 0, turn))
            st2[h, 4] = row_sum[h, ring(b - turn)]
            rs(h, 4, st2.at[h, 4], st2.at[h, 1], along(h, 0, -turn))

    def rs_fourth():
        for h in range(2):
            a, b = axes(h)
            rs_wait(h, 3, st2.at[h, 0])
            st2[h, 5] = row_sum[h, ring(b + turn)] + st2[h, 0]
            rs(h, 5, st2.at[h, 5], st2.at[h, 2], along(h, 0, turn))

    def rs_last():
        for h in range(2):
            a, b = axes(h)
            rs_wait(h, 4, st2.at[h, 1])
            rs_wait(h, 5, st2.at[h, 2])
            total = row_sum[h, b] + st2[h, 1] + st2[h, 2]
            mixed[h * half : (h + 1) * half, :] = total.astype(BF16)

    z_step("out+", 0)
    z_step("out-", 0)
    grad_preact()
    z_step("in+", 0)
    z_step("in-", 0)
    out_partial()
    pair_send()
    pair_add()
    rs_first()
    z_step("out+", 1)
    z_step("out-", 1)
    rs_second()
    z_step("in+", 1)
    z_step("in-", 1)
    rs_third()
    z_step("out+", 2)
    z_step("out-", 2)
    rs_fourth()
    z_step("in+", 2)
    z_step("in-", 2)
    rs_last()
    z_step("out+", 3)
    z_step("in-", 3)
    add_in(z, [], grad_in, 0, in_rows)
    add_out(z, [], grad_out)
    z_copy("out-", 2).wait_recv()
    grad_out[...] += z_out[6].astype(F32)
    for n in range(2):
        z_copy("in+", 2, n).wait_recv()
    grad_in[...] += z_in[2].astype(F32)
    for n in range(2):
        r = slice(n * in_half, (n + 1) * in_half)
        z_copy("in-", 3, n).wait_recv()
        grad_in[r, :] += z_in[6, r].astype(F32)
    z_copy("out+", 3).wait_recv()
    grad_out[...] += z_out[3].astype(F32)
    cot_sent()
    feat_sent()
    remote(part.at[:, : 18 * LANES], part.at[:, : 18 * LANES], rs_send.at[0], rs_recv.at[0], partner).wait_send()
    remote(pair, pair, rs_send.at[1], rs_recv.at[12], partner).wait_send()
    for i, slots in enumerate((z_in, z_out)):
        remote(slots.at[0:7], slots.at[0:7], z_send.at[i], z_recv.at[7 * i], up).wait_send()


def hand_over_kernel(*refs):
    n = (len(refs) - 2) // 3
    ins, outs, held = refs[:n], refs[n : 2 * n], refs[2 * n : 3 * n]
    sem_in, sem_out = refs[3 * n], refs[3 * n + 1]
    pieces = 2
    reads, writes = [], []
    for k in range(n):
        rows = ins[k].shape[0] // pieces
        for p in range(pieces):
            r = pl.ds(p * rows, rows)
            i = k * pieces + p
            reads.append(pltpu.make_async_copy(ins[k].at[r], held[k].at[r], sem_in.at[i]))
            writes.append(pltpu.make_async_copy(held[k].at[r], outs[k].at[r], sem_out.at[i]))
    for c in reads:
        c.start()
    for c, w in zip(reads, writes):
        c.wait()
        w.start()
    for w in writes:
        w.wait()


def hand_over(arrays):
    hbm = pl.BlockSpec(memory_space=pl.ANY)
    n = len(arrays)
    return pl.pallas_call(
        hand_over_kernel,
        out_shape=tuple(jax.ShapeDtypeStruct(a.shape, a.dtype) for a in arrays),
        in_specs=[hbm] * n,
        out_specs=(hbm,) * n,
        scratch_shapes=[pltpu.VMEM(a.shape, a.dtype) for a in arrays]
        + [pltpu.SemaphoreType.DMA((2 * n,)), pltpu.SemaphoreType.DMA((2 * n,))],
    )(*arrays)


def shards(lookup_ids, bag_lengths, feature_widths, tables, w_in, w_out, cotangent):
    samples, bag = lookup_ids.shape[0], lookup_ids.shape[2]
    vocab = tables.shape[1]
    wide_in, hidden = w_in.shape
    wide_out = w_out.shape[1]
    in_rows, out_rows = wide_in // DEPTH, hidden // DEPTH
    half = samples // 2
    vmem = pl.BlockSpec(memory_space=pltpu.VMEM)
    hbm = pl.BlockSpec(memory_space=pl.ANY)
    dma = pltpu.SemaphoreType.DMA
    outs = pl.pallas_call(
        kernel,
        out_shape=(
            jax.ShapeDtypeStruct((samples, LANES), BF16),
            jax.ShapeDtypeStruct((in_rows, hidden), F32),
            jax.ShapeDtypeStruct((out_rows, wide_out), F32),
        ),
        in_specs=[pl.BlockSpec(memory_space=pltpu.SMEM), vmem, vmem, hbm, hbm, hbm, hbm],
        out_specs=(vmem, vmem, vmem),
        scratch_shapes=[
            pltpu.VMEM((vocab, LANES), BF16),
            pltpu.VMEM((wide_in, hidden), BF16),
            pltpu.VMEM((hidden, wide_out), BF16),
            pltpu.VMEM((samples, wide_out), BF16),
            pltpu.VMEM((samples, wide_in), BF16),
            pltpu.VMEM((samples, bag), jnp.int32),
            pltpu.VMEM((samples, 8), F32),
            pltpu.VMEM((2, samples // PIECES, vocab), BF16),
            pltpu.VMEM((samples, hidden), F32),
            pltpu.VMEM((samples, hidden), F32),
            pltpu.VMEM((samples, hidden), BF16),
            pltpu.VMEM((hidden, samples), BF16),
            pltpu.VMEM((samples, hidden), BF16),
            pltpu.VMEM((samples, wide_out), BF16),
            pltpu.VMEM((SIDE * SIDE, samples, LANES), BF16),
            pltpu.VMEM((2, 3, SIDE, half, LANES), BF16),
            pltpu.VMEM((2, 6, half, LANES), F32),
            pltpu.VMEM((2, SIDE, half, LANES), F32),
            pltpu.VMEM((9, in_rows, hidden), BF16),
            pltpu.VMEM((9, out_rows, wide_out), BF16),
            dma((4,)),
            dma((2,)),
            dma((32,)),
            dma((2,)),
            dma((13,)),
            dma((2,)),
            dma((21,)),
        ],
        compiler_params=pltpu.CompilerParams(
            collective_id=0, has_side_effects=True, vmem_limit_bytes=63 * 1024 * 1024
        ),
    )(
        feature_widths, jnp.transpose(lookup_ids[:, 0, :]), jnp.transpose(bag_lengths), tables[0], w_in, w_out, cotangent
    )
    return hand_over(outs)


def solution(mesh):
    return jax.shard_map(
        shards,
        mesh=mesh,
        in_specs=(
            P("dp", "table", None),
            P("dp", "table"),
            P(),
            P("table", None, "tensor"),
            P(None, ("table", "tensor")),
            P(("table", "tensor"), None),
            P("dp", ("table", "tensor")),
        ),
        out_specs=(
            P("dp", ("table", "tensor")),
            P("dp", ("table", "tensor")),
            P(("table", "tensor", "dp"), None),
        ),
        check_vma=False,
    )
```

```python
import functools

import jax
import jax.numpy as jnp
from jax import lax
from jax.experimental import pallas as pl
from jax.experimental.pallas import tpu as pltpu
from jax.sharding import PartitionSpec as P

MESH = pl.DeviceIdType.MESH
F32, BF16 = jnp.float32, jnp.bfloat16
SIDE = 4
DEPTH = 8
LANES = 128
TILE = 512
PLAN_BEFORE = ((), (), (), (0, 1), (), (2,), (3,), ())
PLAN_AFTER = ((0, 4), (1, 0), (0, 5), (1, 1), (0, 6), (1, 2), (1, 3), (0, 7), (1, 4), (1, 5), (1, 6), (0, 8), (1, 7))
PIECES = 8
FIELDS = 4


def mul128(i):
    return pl.multiple_of(i * LANES, LANES)


def kernel(
    widths, ids, lens, table_hbm, w_in_hbm, w_out_hbm, cot_hbm,
    mixed_hbm, grad_in_hbm, grad_out_hbm,
    mixed, grad_in, grad_out,
    table, w_in, w_out, cot, feat, keys, spans, counts, gh, pre, hid, hid_t, gp,
    part, pair, st1, st2, row_sum, z_in, z_out,
    in_sem, out_sem, ag_send, ag_recv, rs_send, rs_recv, z_send, z_recv,
):
    t, yh, z = lax.axis_index("table"), lax.axis_index("tensor"), lax.axis_index("dp")
    core = lax.rem(t, 2)
    x = lax.rem(lax.div(t, 2), SIDE)
    y = yh * 2 + lax.div(t, 2 * SIDE)
    turn = 1 - 2 * core
    bag, samples = ids.shape
    half = samples // 2

    def ring(i):
        return lax.rem(i + 2 * SIDE, SIDE)

    def ring_z(i):
        return lax.rem(i + 2 * DEPTH, DEPTH)

    def dev(px, py, c, pz):
        return {"table": (lax.rem(py, 2) * SIDE + px) * 2 + c, "tensor": lax.div(py, 2), "dp": pz}

    def block(px, py, c):
        return ((lax.rem(py, 2) * SIDE + px) * 2 + c) * 2 + lax.div(py, 2)

    def place(h, a, b):
        return (a, b) if h == 0 else (b, a)

    first = (x, y)
    second = (y, x)

    def peer(h, a, b):
        px, py = place(h, a, b)
        return dev(px, py, core, z)

    partner = dev(x, y, 1 - core, z)

    loads = [
        pltpu.make_async_copy(cot_hbm, cot.at[:, pl.ds(mul128(block(x, y, core)), LANES)], in_sem.at[0]),
        pltpu.make_async_copy(table_hbm, table, in_sem.at[1]),
        pltpu.make_async_copy(w_out_hbm, w_out, in_sem.at[2]),
        pltpu.make_async_copy(w_in_hbm, w_in, in_sem.at[3]),
    ]
    for load in loads:
        load.start()

    barrier = pltpu.get_barrier_semaphore()
    neighbours = [
        dev(ring(x + 1), y, core, z), dev(ring(x - 1), y, core, z),
        dev(x, ring(y + 1), core, z), dev(x, ring(y - 1), core, z),
        dev(ring(x + 2), y, core, z), dev(x, ring(y + 2), core, z),
        dev(x, y, core, ring_z(z + 1)), dev(x, y, core, ring_z(z - 1)), partner,
    ]
    for neighbour in neighbours:
        pl.semaphore_signal(barrier, inc=1, device_id=neighbour, device_id_type=MESH)

    def remote(src, dst, s, r, to):
        return pltpu.make_async_remote_copy(
            src_ref=src, dst_ref=dst, send_sem=s, recv_sem=r, device_id=to, device_id_type=MESH
        )

    def gather(which, buf, row, rows):
        def view(h, a, b, c):
            px, py = place(h, a, b)
            return buf.at[pl.ds(row + h * (rows // 2), rows // 2), pl.ds(mul128(block(px, py, c)), LANES)]

        def copy(h, a, b, recv_slot, to):
            ref = view(h, a, b, core)
            remote(ref, ref, ag_send.at[which], ag_recv.at[which * 16 + recv_slot], to).start()

        def arrived(recv_slot, blocks=1):
            ref = buf.at[:rows, : blocks * LANES]
            remote(ref, ref, ag_send.at[which], ag_recv.at[which * 16 + recv_slot], partner).wait_recv()

        def sent():
            ref = buf.at[:rows, : 31 * LANES]
            remote(ref, ref, ag_send.at[which], ag_recv.at[which * 16], partner).wait_send()

        def to_partner(h, a, b):
            copy(h, a, b, 15, partner)

        def offset(j):
            return (0, -turn, turn, 2)[j]

        def line(h, j):
            a, b = first[h], second[h]
            aj = ring(a + offset(j))
            copy(h, aj, b, 3 + 3 * j + core, peer(h, a, ring(b + turn)))
            copy(h, aj, b, 3 + 3 * j + (1 - core), peer(h, a, ring(b - turn)))

        def begin():
            for h in range(2):
                a, b = first[h], second[h]
                copy(h, a, b, core, peer(h, ring(a + turn), b))
                copy(h, a, b, 1 - core, peer(h, ring(a - turn), b))
                copy(h, a, b, 2, peer(h, ring(a + 2), b))
            for h in range(2):
                line(h, 0)
                to_partner(h, first[h], second[h])

        def near():
            arrived(core)
            for h in range(2):
                a, b = first[h], second[h]
                aj = ring(a - turn)
                line(h, 1)
                to_partner(h, aj, b)

        def other():
            arrived(1 - core)
            for h in range(2):
                line(h, 2)
                to_partner(h, ring(first[h] + turn), second[h])

        def far():
            arrived(2)
            for h in range(2):
                line(h, 3)
                to_partner(h, ring(first[h] + 2), second[h])

        def cross(j):
            arrived(3 + 3 * j + core)
            for h in range(2):
                a, b = first[h], second[h]
                aj, bj = ring(a + offset(j)), ring(b - turn)
                copy(h, aj, bj, 5 + 3 * j, peer(h, a, ring(b + turn)))
                to_partner(h, aj, bj)
            arrived(3 + 3 * j + (1 - core))
            for h in range(2):
                to_partner(h, ring(first[h] + offset(j)), ring(second[h] + turn))

        def cross_far(j):
            arrived(5 + 3 * j)
            for h in range(2):
                to_partner(h, ring(first[h] + offset(j)), ring(second[h] + 2))

        steps = [
            near,
            other,
            far,
            lambda: cross(0),
            lambda: cross(1),
            lambda: cross(2),
            lambda: cross(3),
            lambda: [cross_far(j) for j in range(4)],
            lambda: arrived(15, 16),
        ]
        return begin, steps, sent

    vocab = table.shape[0]
    words = vocab // FIELDS

    def spread():
        inside = lax.broadcasted_iota(jnp.int32, (bag, samples), 0) < lens[...]
        field = lax.shift_right_logical(ids[...], words.bit_length() - 1)
        code = lax.bitwise_and(ids[...], words - 1) + field * (8 << 16)
        keys[...] = jnp.transpose(jnp.where(inside, code, 2 * words))

        spans[...] = jnp.transpose(jnp.broadcast_to(lens[...], (8, samples)).astype(F32))

    piece = counts.shape[1]

    def count(n):
        rows = 8
        lane = lax.broadcasted_iota(jnp.int32, (rows, LANES), 1)
        for g in range(0, piece, rows):
            code = keys[n * piece + g : n * piece + g + rows, :]
            spread_keys, spread_units = [], []
            for b in range(bag):
                wide = jnp.broadcast_to(code[:, b : b + 1], (rows, LANES))
                spread_keys.append(lax.bitwise_and(wide, 0xFFFF))
                spread_units.append(lax.shift_left(jnp.ones_like(wide), lax.shift_right_logical(wide, 16)))
            for w in range(0, words, LANES):
                target = lane + w
                parts = []
                for b in range(bag):
                    parts.append(jnp.where(spread_keys[b] == target, spread_units[b], 0))
                while len(parts) > 1:
                    parts = [p + q for p, q in zip(parts[::2], parts[1::2])]
                for f in range(FIELDS):
                    number = lax.bitwise_and(lax.shift_right_logical(parts[0], 8 * f), 255)
                    at = f * words + w
                    counts[n % 2, g : g + rows, at : at + LANES] = number.astype(F32).astype(BF16)

    def pool_end(n):
        r = slice(n * piece, (n + 1) * piece)
        summed = jnp.dot(counts[n % 2], table[...], preferred_element_type=F32)
        mean = summed / spans[r, 0:1]
        column = lax.broadcasted_iota(jnp.int32, (piece, LANES), 1) + yh * LANES
        mean = jnp.where(column < widths[t], mean, jnp.zeros_like(mean))
        feat[r, pl.ds(mul128(block(x, y, core)), LANES)] = mean.astype(BF16)

    def grad_hidden(low, high):
        @pl.loop(low, high)
        def _(k):
            cols = pl.ds(pl.multiple_of(k * TILE, TILE), TILE)
            gh[...] += lax.dot_general(
                cot[:, cols], w_out[:, cols], (((1,), (1,)), ((), ())), preferred_element_type=F32
            )

    def preact(parity):
        width = 4 * LANES // 2

        @pl.loop(0, feat.shape[1] // (2 * width))
        def _(k):
            cols = pl.ds(pl.multiple_of((2 * k + parity) * width, width), width)
            pre[...] += jnp.dot(feat[:, cols], w_in[cols, :], preferred_element_type=F32)

    begin_cot, cot_steps, cot_sent = gather(0, cot, 0, samples)
    begin_feat, feat_steps, feat_sent = gather(1, feat, 0, samples)
    tiles = cot.shape[1] // TILE
    spread()
    gh[...] = jnp.zeros_like(gh)
    pre[...] = jnp.zeros_like(pre)
    for n in range(PIECES):
        count(n)
        if n == 0:
            loads[1].wait()
            pl.semaphore_wait(barrier, len(neighbours))
            loads[0].wait()
            begin_cot()
        else:
            pool_end(n - 1)
        for k in PLAN_BEFORE[n]:
            cot_steps[k]()
    pool_end(PIECES - 1)
    begin_feat()
    loads[2].wait()
    for which, n in PLAN_AFTER:
        (cot_steps, feat_steps)[which][n]()
    loads[3].wait()
    preact(core)
    feat_steps[8]()
    preact(1 - core)

    rows = 64

    @pl.loop(0, samples // rows)
    def _(i):
        r = pl.ds(pl.multiple_of(i * rows, rows), rows)
        value = pre[r, :]
        gate = jax.nn.sigmoid(value)
        hid[r, :] = (value * gate).astype(BF16)
        pre[r, :] = gate * (1.0 + value * (1.0 - gate))

    hid_t[...] = jnp.transpose(hid[...])

    def grad_preact():
        grad_hidden(0, tiles)

        @pl.loop(0, samples // rows)
        def _(i):
            r = pl.ds(pl.multiple_of(i * rows, rows), rows)
            gp[r, :] = (gh[r, :] * pre[r, :]).astype(BF16)

    in_rows, in_cols = grad_in.shape
    out_rows, out_cols = grad_out.shape

    def add_in(d, terms, store, low, high):
        step = 128

        @pl.loop(low // step, high // step)
        def _(i):
            r = pl.ds(pl.multiple_of(i * step, step), step)
            cols = pl.ds(pl.multiple_of(d * in_rows + i * step, step), step)
            own = lax.dot_general(feat[:, cols], gp[...], (((0,), (0,)), ((), ())), preferred_element_type=F32)
            for term in terms:
                own = own + term[r, :].astype(F32)
            store[r, :] = own.astype(store.dtype)

    def add_out(d, terms, store):
        @pl.loop(0, out_cols // TILE)
        def _(j):
            cols = pl.ds(pl.multiple_of(j * TILE, TILE), TILE)
            lhs = hid_t[pl.ds(pl.multiple_of(d * out_rows, out_rows), out_rows), :]
            own = jnp.dot(lhs, cot[:, cols], preferred_element_type=F32)
            for term in terms:
                own = own + term[:, cols].astype(F32)
            store[:, cols] = own.astype(store.dtype)

    up, down = dev(x, y, core, ring_z(z + 1)), dev(x, y, core, ring_z(z - 1))
    chains = {"out+": (0, 4, 1), "out-": (4, 3, -1), "in+": (0, 3, 1), "in-": (3, 4, -1)}
    in_half = in_rows // 2

    def start_slot(name):
        return 7 + (0 if name.endswith("+") else 1)

    def z_copy(name, s, n=0):
        slot, hops, sign = chains[name]
        from_slot = start_slot(name) if s == 0 else slot + s - 1
        to = up if sign > 0 else down
        if name[:3] == "out":
            return remote(z_out.at[from_slot], z_out.at[slot + s], z_send.at[1], z_recv.at[14 + slot + s], to)
        r = pl.ds(n * in_half, in_half)
        return remote(z_in.at[from_slot, r], z_in.at[slot + s, r], z_send.at[0], z_recv.at[n * 7 + slot + s], to)

    def z_step(name, s):
        slot, hops, sign = chains[name]
        d = ring_z(z + sign * (hops - s))
        for n in range(1 if name[:3] == "out" else 2):
            if s > 0:
                z_copy(name, s - 1, n).wait_recv()
            from_slot = start_slot(name) if s == 0 else slot + s - 1
            slots = z_out if name[:3] == "out" else z_in
            terms = [slots.at[from_slot]] if s > 0 else []
            if name[:3] == "out":
                add_out(d, terms, slots.at[from_slot])
            else:
                add_in(d, terms, slots.at[from_slot], n * in_half, (n + 1) * in_half)
            z_copy(name, s, n).start()

    def rs(h, n, src, dst, to):
        remote(src, dst, rs_send.at[0], rs_recv.at[h * 6 + n], to).start()

    def rs_wait(h, n, ref):
        remote(ref, ref, rs_send.at[0], rs_recv.at[h * 6 + n], partner).wait_recv()

    def cols_of(px, py, c):
        return pl.ds(mul128(block(px, py, c)), LANES)

    def out_partial():
        @pl.loop(0, part.shape[1] // TILE)
        def _(j):
            cols = pl.ds(pl.multiple_of(j * TILE, TILE), TILE)
            part[:, cols] = jnp.dot(hid[...], w_out[:, cols], preferred_element_type=F32).astype(BF16)

    def pair_send():
        for n in range(SIDE * SIDE):
            px, py = divmod(n, SIDE)
            remote(part.at[:, cols_of(px, py, 1 - core)], pair.at[n], rs_send.at[1], rs_recv.at[12], partner).start()

    def pair_add():
        remote(pair, pair, rs_send.at[1], rs_recv.at[12], partner).wait_recv()

        @pl.loop(0, SIDE * SIDE)
        def _(n):
            px, py = lax.div(n, SIDE), lax.rem(n, SIDE)
            both = part[:, cols_of(px, py, core)].astype(F32) + pair[n].astype(F32)
            pair[n] = both.astype(BF16)

    def chip(h, a, b):
        px, py = (b, a) if h == 0 else (a, b)
        return pair.at[px * SIDE + py, pl.ds(h * half, half), :]

    def along(h, da, db):
        if h == 0:
            return dev(ring(x + db), ring(y + da), core, z)
        return dev(ring(x + da), ring(y + db), core, z)

    def axes(h):
        return (y, x) if h == 0 else (x, y)

    def rs_first():
        for h in range(2):
            a, b = axes(h)
            for k in range(SIDE):
                rs(h, 0, chip(h, ring(a + 2), k), st1.at[h, 0, k], along(h, turn, 0))
                rs(h, 1, chip(h, ring(a - turn), k), st1.at[h, 1, k], along(h, -turn, 0))

    def rs_second():
        for h in range(2):
            a, b = axes(h)
            rs_wait(h, 0, st1.at[h, 0])
            for k in range(SIDE):
                own = chip(h, ring(a + turn), k)[...].astype(F32)
                st1[h, 0, k] = (own + st1[h, 0, k].astype(F32)).astype(BF16)
                rs(h, 2, st1.at[h, 0, k], st1.at[h, 2, k], along(h, turn, 0))

    def rs_third():
        for h in range(2):
            a, b = axes(h)
            rs_wait(h, 1, st1.at[h, 1])
            rs_wait(h, 2, st1.at[h, 2])
            for k in range(SIDE):
                own = chip(h, a, k)[...].astype(F32)
                row_sum[h, k] = own + st1[h, 1, k].astype(F32) + st1[h, 2, k].astype(F32)
            st2[h, 3] = row_sum[h, ring(b + 2)]
            rs(h, 3, st2.at[h, 3], st2.at[h, 0], along(h, 0, turn))
            st2[h, 4] = row_sum[h, ring(b - turn)]
            rs(h, 4, st2.at[h, 4], st2.at[h, 1], along(h, 0, -turn))

    def rs_fourth():
        for h in range(2):
            a, b = axes(h)
            rs_wait(h, 3, st2.at[h, 0])
            st2[h, 5] = row_sum[h, ring(b + turn)] + st2[h, 0]
            rs(h, 5, st2.at[h, 5], st2.at[h, 2], along(h, 0, turn))

    def rs_last():
        for h in range(2):
            a, b = axes(h)
            rs_wait(h, 4, st2.at[h, 1])
            rs_wait(h, 5, st2.at[h, 2])
            total = row_sum[h, b] + st2[h, 1] + st2[h, 2]
            mixed[h * half : (h + 1) * half, :] = total.astype(BF16)

    z_step("out+", 0)
    z_step("out-", 0)
    grad_preact()
    z_step("in+", 0)
    z_step("in-", 0)
    out_partial()
    pair_send()
    pair_add()
    rs_first()
    z_step("out+", 1)
    z_step("out-", 1)
    rs_second()
    z_step("in+", 1)
    z_step("in-", 1)
    rs_third()
    z_step("out+", 2)
    z_step("out-", 2)
    rs_fourth()
    z_step("in+", 2)
    z_step("in-", 2)
    rs_last()
    mixed_out = pltpu.make_async_copy(mixed, mixed_hbm, out_sem.at[0])
    mixed_out.start()
    z_step("out+", 3)
    z_step("in-", 3)
    add_in(z, [], grad_in, 0, in_rows)
    add_out(z, [], grad_out)
    z_copy("out-", 2).wait_recv()
    grad_out[...] += z_out[6].astype(F32)
    for n in range(2):
        z_copy("in+", 2, n).wait_recv()
    grad_in[...] += z_in[2].astype(F32)
    leaving = [mixed_out]
    for n in range(2):
        r = pl.ds(n * in_half, in_half)
        z_copy("in-", 3, n).wait_recv()
        grad_in[r, :] += z_in[6, r].astype(F32)
        leaving.append(pltpu.make_async_copy(grad_in.at[r], grad_in_hbm.at[r], out_sem.at[1 + n]))
        leaving[-1].start()
    z_copy("out+", 3).wait_recv()
    grad_out[...] += z_out[3].astype(F32)
    leaving.append(pltpu.make_async_copy(grad_out, grad_out_hbm, out_sem.at[3]))
    leaving[-1].start()
    cot_sent()
    feat_sent()
    remote(part.at[:, : 18 * LANES], part.at[:, : 18 * LANES], rs_send.at[0], rs_recv.at[0], partner).wait_send()
    remote(pair, pair, rs_send.at[1], rs_recv.at[12], partner).wait_send()
    for i, slots in enumerate((z_in, z_out)):
        remote(slots.at[0:7], slots.at[0:7], z_send.at[i], z_recv.at[7 * i], up).wait_send()
    for c in leaving:
        c.wait()


def hand_over_kernel(*refs):
    n = (len(refs) - 2) // 3
    ins, outs, held = refs[:n], refs[n : 2 * n], refs[2 * n : 3 * n]
    sem_in, sem_out = refs[3 * n], refs[3 * n + 1]
    pieces = 2
    reads, writes = [], []
    for k in range(n):
        rows = ins[k].shape[0] // pieces
        for p in range(pieces):
            r = pl.ds(p * rows, rows)
            i = k * pieces + p
            reads.append(pltpu.make_async_copy(ins[k].at[r], held[k].at[r], sem_in.at[i]))
            writes.append(pltpu.make_async_copy(held[k].at[r], outs[k].at[r], sem_out.at[i]))
    for c in reads:
        c.start()
    for c, w in zip(reads, writes):
        c.wait()
        w.start()
    for w in writes:
        w.wait()


def hand_over(arrays):
    hbm = pl.BlockSpec(memory_space=pl.ANY)
    n = len(arrays)
    return pl.pallas_call(
        hand_over_kernel,
        out_shape=tuple(jax.ShapeDtypeStruct(a.shape, a.dtype) for a in arrays),
        in_specs=[hbm] * n,
        out_specs=(hbm,) * n,
        scratch_shapes=[pltpu.VMEM(a.shape, a.dtype) for a in arrays]
        + [pltpu.SemaphoreType.DMA((2 * n,)), pltpu.SemaphoreType.DMA((2 * n,))],
    )(*arrays)


def shards(lookup_ids, bag_lengths, feature_widths, tables, w_in, w_out, cotangent):
    samples, bag = lookup_ids.shape[0], lookup_ids.shape[2]
    vocab = tables.shape[1]
    wide_in, hidden = w_in.shape
    wide_out = w_out.shape[1]
    in_rows, out_rows = wide_in // DEPTH, hidden // DEPTH
    half = samples // 2
    vmem = pl.BlockSpec(memory_space=pltpu.VMEM)
    hbm = pl.BlockSpec(memory_space=pl.ANY)
    dma = pltpu.SemaphoreType.DMA
    outs = pl.pallas_call(
        kernel,
        out_shape=(
            jax.ShapeDtypeStruct((samples, LANES), BF16),
            jax.ShapeDtypeStruct((in_rows, hidden), F32),
            jax.ShapeDtypeStruct((out_rows, wide_out), F32),
        ),
        in_specs=[pl.BlockSpec(memory_space=pltpu.SMEM), vmem, vmem, hbm, hbm, hbm, hbm],
        out_specs=(hbm, hbm, hbm),
        scratch_shapes=[
            pltpu.VMEM((samples, LANES), BF16),
            pltpu.VMEM((in_rows, hidden), F32),
            pltpu.VMEM((out_rows, wide_out), F32),
            pltpu.VMEM((vocab, LANES), BF16),
            pltpu.VMEM((wide_in, hidden), BF16),
            pltpu.VMEM((hidden, wide_out), BF16),
            pltpu.VMEM((samples, wide_out), BF16),
            pltpu.VMEM((samples, wide_in), BF16),
            pltpu.VMEM((samples, bag), jnp.int32),
            pltpu.VMEM((samples, 8), F32),
            pltpu.VMEM((2, samples // PIECES, vocab), BF16),
            pltpu.VMEM((samples, hidden), F32),
            pltpu.VMEM((samples, hidden), F32),
            pltpu.VMEM((samples, hidden), BF16),
            pltpu.VMEM((hidden, samples), BF16),
            pltpu.VMEM((samples, hidden), BF16),
            pltpu.VMEM((samples, wide_out), BF16),
            pltpu.VMEM((SIDE * SIDE, samples, LANES), BF16),
            pltpu.VMEM((2, 3, SIDE, half, LANES), BF16),
            pltpu.VMEM((2, 6, half, LANES), F32),
            pltpu.VMEM((2, SIDE, half, LANES), F32),
            pltpu.VMEM((9, in_rows, hidden), BF16),
            pltpu.VMEM((9, out_rows, wide_out), BF16),
            dma((4,)),
            dma((4,)),
            dma((2,)),
            dma((32,)),
            dma((2,)),
            dma((13,)),
            dma((2,)),
            dma((21,)),
        ],
        compiler_params=pltpu.CompilerParams(
            collective_id=0, has_side_effects=True, vmem_limit_bytes=63 * 1024 * 1024
        ),
    )(
        feature_widths, jnp.transpose(lookup_ids[:, 0, :]), jnp.transpose(bag_lengths), tables[0], w_in, w_out, cotangent
    )
    return hand_over(outs)


def solution(mesh):
    return jax.shard_map(
        shards,
        mesh=mesh,
        in_specs=(
            P("dp", "table", None),
            P("dp", "table"),
            P(),
            P("table", None, "tensor"),
            P(None, ("table", "tensor")),
            P(("table", "tensor"), None),
            P("dp", ("table", "tensor")),
        ),
        out_specs=(
            P("dp", ("table", "tensor")),
            P("dp", ("table", "tensor")),
            P(("table", "tensor", "dp"), None),
        ),
        check_vma=False,
    )
```
